512 devices in a mesh: level: 128 (over z, y_hi, x), sample: 4 (over y_lo, core).
Axes of the slice: x: 4, y: 4 (y_hi: 2, y_lo: 2; y = y_hi * 2 + y_lo), z: 16, core: 2. Of those that a mesh axis runs over, the one named last changes fastest.
Arguments:
- samples: bfloat16 [524288, 512], P('level', 'sample'), may hold values from -6 to 6
- sketch: bfloat16 [2, 128, 256], replicated, may hold values from -0.375 to 0.375
Outputs:
- far_factors: float32 [2048, 128, 128], P('level')
- near_factors: float32 [1024, 128, 128], P('level')
- basis_rows: float32 [131072, 512], P('level', 'sample')
The draws below stay inside these ranges and needn't reach their ends.
All inputs are finite; a program needn't handle non-finite values.
Results may differ from the reference program's by a relative error of at most 0.0031.
Values may be sent and summed in bfloat16 or wider, within the bound.
No kernel may reach another device: no remote copies, remote signals or barrier semaphores. Data moves between devices by JAX's collectives and lax.ppermute only.
A program may use at most 64 MiB of HBM per device.

```python
import math
import jax
import jax.numpy as jnp
from jax import lax

RANK = 128
SAMPLES = 512
ROWS_DEV = 4096
ORDER = 524288
N_LEVEL = 128


def levels(key, dims, pieces, low, largest):
    def one(dim, blocks):
        draws = jax.random.uniform(jax.random.fold_in(jax.random.fold_in(key, 6), dim), (blocks,), jnp.float32, low / len(pieces), largest / len(pieces))
        return jnp.repeat(jnp.exp(draws), dims[dim] // blocks).reshape((-1,) + (1,) * (len(dims) - dim - 1))

    gain = one(*pieces[0])
    for cut in pieces[1:]:
        gain = gain * one(*cut)
    return gain


def gaussian(stream_key, extent, width, most, split=(), held_as=jnp.bfloat16):
    entries = width * jax.random.normal(stream_key, extent, jnp.float32)
    if split:
        entries = entries * levels(stream_key, extent, split, -0.22, 0.18)
    return jnp.clip(entries, -most, most).astype(held_as)


def setup_inputs(seed: int = 0) -> dict:
    arg_keys = jax.random.split(jax.random.key(seed), 3)
    samples = gaussian(arg_keys[0], (ORDER, SAMPLES), 1.0, 6.0, ((0, 128), (1, 4)))
    sketch = gaussian(arg_keys[1], (2, RANK, 2 * RANK), (2 * RANK) ** -0.5, 0.375)
    return dict(samples=samples, sketch=sketch)


def level_step(rows, sketch_level, distance):
    groups = rows.shape[0]
    half = rows.shape[1] // 2
    columns = rows.shape[2]
    index = jnp.arange(groups, dtype=jnp.int32)
    partner = rows[jnp.bitwise_xor(index, distance)]
    upper = (index // distance % 2 == 1)[:, None, None]
    lower_rows = jnp.where(upper, partner[:, half:], rows[:, :half])
    upper_rows = jnp.where(upper, rows[:, half:], partner[:, :half])
    boxes = half // RANK
    left = sketch_level[:, :RANK].astype(jnp.float32)
    right = sketch_level[:, RANK:].astype(jnp.float32)

    def one_group(pair):
        first = pair[0].reshape(boxes, RANK, columns).astype(jnp.float32)
        second = pair[1].reshape(boxes, RANK, columns).astype(jnp.float32)
        projected = jnp.einsum('rm,bmc->brc', left, first) + jnp.einsum('rm,bmc->brc', right, second)
        gram = jnp.einsum('brc,bsc->brs', projected, projected, precision=lax.Precision.HIGHEST)
        factor = jnp.linalg.cholesky(gram)

        def solve_box(factor_box, block_box):
            return jax.scipy.linalg.solve_triangular(factor_box, block_box, lower=True)
        solved = jax.vmap(solve_box)(factor, projected) * math.sqrt(SAMPLES)
        return (factor, solved.reshape(boxes * RANK, columns))
    return lax.map(one_group, (lower_rows, upper_rows))

def reference(samples, sketch):
    columns = samples.shape[1]
    rows = samples.reshape(N_LEVEL, ROWS_DEV, columns)
    far, first = level_step(rows, sketch[0], N_LEVEL // 2)
    first = first.astype(jnp.bfloat16)
    near, second = level_step(first, sketch[1], 1)
    return (far.reshape(-1, RANK, RANK), near.reshape(-1, RANK, RANK), second.reshape(-1, columns))
```

```python
import functools
import math
import jax
import jax.numpy as jnp
from jax import lax
from jax.experimental import pallas as pl
from jax.experimental.pallas import tpu as pltpu
from jax.sharding import Mesh, PartitionSpec as P

RANK = 128
B = 16
F32 = jnp.float32
BF16 = jnp.bfloat16


def split3(x):
    h = x.astype(BF16)
    r = x - h.astype(F32)
    m = r.astype(BF16)
    l = (r - m.astype(F32)).astype(BF16)
    return h, m, l


def dot_nn(a, b):
    return lax.dot_general(a, b, (((1,), (0,)), ((), ())), preferred_element_type=F32)


def dot_nt(a, b):
    return lax.dot_general(a, b, (((1,), (1,)), ((), ())), preferred_element_type=F32)


def take_lanes(x, index):
    return jnp.take_along_axis(x, index, axis=1)


def leaf(rows, lane, sub):
    rows = list(rows)
    for k in range(B):
        half, at = divmod(k, 8)
        here = sub == at
        pivot = rows[k][half][at:at + 1, :]
        r = lax.rsqrt(pivot)
        u = [part * r for part in rows[k]]
        full = list(u)
        full[half] = jnp.where(here, r, u[half])
        rows[k] = full
        for i in range(k + 1, B):
            ui = u[i // 8][i % 8:i % 8 + 1, :]
            new = []
            for t in range(2):
                old = rows[i][t]
                if t == half:
                    old = jnp.where(here, 0.0, old)
                new.append(old - ui * full[t])
            rows[i] = new
    out = [rows[0][0], rows[0][1]]
    for i in range(1, B):
        sel = (lane % B) == i
        out = [jnp.where(sel, rows[i][t], out[t]) for t in range(2)]
    return out


def factor(f_refs, boxes):
    lane = lax.broadcasted_iota(jnp.int32, (8, RANK), 1)
    sub = lax.broadcasted_iota(jnp.int32, (8, RANK), 0)
    lane_big = lax.broadcasted_iota(jnp.int32, (RANK, RANK), 1)
    row_big = lax.broadcasted_iota(jnp.int32, (RANK, RANK), 0)
    seg = lane // B
    for p in range(RANK // B):
        lo = B * p
        cat = [None, None]
        for b in range(boxes):
            for t in range(2):
                tile = f_refs[b][lo + 8 * t:lo + 8 * t + 8, :]
                rep = take_lanes(tile, lo + lane % B)
                cat[t] = rep if b == 0 else jnp.where(seg % boxes == b, rep, cat[t])
        rows = []
        for i in range(B):
            idx = seg * B + i
            rows.append([take_lanes(cat[t], idx) for t in range(2)])
        out = leaf(rows, lane, sub)
        q_big = lane_big // B
        for b in range(boxes):
            idx = b * B + lane % B
            rep = [take_lanes(out[t], idx) for t in range(2)]
            full = jnp.concatenate(rep, axis=0)
            r16 = lax.broadcasted_iota(jnp.int32, (B, RANK), 0)
            l16 = lax.broadcasted_iota(jnp.int32, (B, RANK), 1)
            wt = jnp.where(r16 <= l16 % B, full, 0.0)
            old = f_refs[b][...]
            if p == RANK // B - 1 and p == 0:
                continue
            pieces = []
            if lo > 0:
                pieces.append(jnp.zeros((lo, RANK), F32))
            pieces.append(wt)
            if lo + B < RANK:
                pieces.append(jnp.zeros((RANK - lo - B, RANK), F32))
            t_full = jnp.concatenate(pieces, axis=0)
            th, tm, tl = split3(t_full)
            fh, fm, fl = split3(old)
            prod = dot_nn(jnp.concatenate([fh, fm], axis=1), jnp.concatenate([th, th], axis=0))
            prod += dot_nn(jnp.concatenate([fh, fm], axis=1), jnp.concatenate([tm, tm], axis=0))
            prod += dot_nn(jnp.concatenate([fh, fl], axis=1), jnp.concatenate([tl, th], axis=0))
            pieces = []
            if lo > 0:
                pieces.append(prod[:lo])
            pieces.append(wt)
            if lo + B < RANK:
                pieces.append(prod[lo + B:])
            panel = jnp.concatenate(pieces, axis=0)
            pieces[1 if lo > 0 else 0] = full
            shown = jnp.concatenate(pieces, axis=0)
            in_block = q_big == p
            base = jnp.where(in_block, shown, old)
            if p < RANK // B - 1:
                h, m, l = (v.astype(F32) for v in split3(panel))
                x = jnp.where((q_big == 0) | (q_big == 1) | (q_big == 3), h,
                              jnp.where((q_big == 2) | (q_big == 5), m,
                                        jnp.where(q_big == 4, l, 0.0))).astype(BF16)
                y = jnp.where((q_big == 0) | (q_big == 2) | (q_big == 4), h,
                              jnp.where((q_big == 1) | (q_big == 5), m,
                                        jnp.where(q_big == 3, l, 0.0)))
                y = jnp.where(row_big >= lo + B, y, 0.0).astype(BF16)
                own = (row_big >= lo) & (row_big < lo + B) & (q_big > p)
                base = jnp.where(own, 0.0, base) - dot_nt(x, y)
            f_refs[b][...] = base


def body(boxes, split_columns, x_ref, s_ref, q_ref, l_ref, z_ref, f_ref):
    s = s_ref[...]
    parts = 512 // RANK
    for b in range(boxes):
        for c in range(parts):
            if split_columns:
                both = jnp.concatenate([x_ref[0, c, b], x_ref[1, c, b]], axis=0)
            else:
                cols = slice(c * RANK, (c + 1) * RANK)
                both = jnp.concatenate([x_ref[0, b, :, cols], x_ref[1, b, :, cols]], axis=0)
            z_ref[b, :, c * RANK:(c + 1) * RANK] = dot_nn(s, both)
        h, m, l = split3(z_ref[b])
        hm = jnp.concatenate([h, m], axis=0)
        p1 = dot_nt(h, hm)
        p2 = dot_nt(m, hm)
        g = p1[:, :RANK] + ((p1[:, RANK:] + p2[:, :RANK]) + (dot_nt(l, h) + dot_nt(h, l)) + p2[:, RANK:])
        f_ref[b] = g
    factor([f_ref.at[b] for b in range(boxes)], boxes)
    row = lax.broadcasted_iota(jnp.int32, (RANK, RANK), 0)
    col = lax.broadcasted_iota(jnp.int32, (RANK, RANK), 1)
    for b in range(boxes):
        f = f_ref[b]
        l_ref[b] = jnp.where(row > col, f, jnp.where(row == col, 1.0 / f, 0.0)).astype(l_ref.dtype)
        w = jnp.where(row <= col, f, 0.0).T * math.sqrt(512)
        wh, wm, wl = split3(w)
        zh, zm, zl = split3(z_ref[b])
        q = dot_nn(jnp.concatenate([wh, wm], axis=1), jnp.concatenate([zh, zh], axis=0))
        q += dot_nn(wh, zm)
        if split_columns:
            q_ref[b] = q.astype(q_ref.dtype)
        else:
            for c in range(parts):
                q_ref[c, b] = q[:, c * RANK:(c + 1) * RANK].astype(q_ref.dtype)


def level1(x, s):
    boxes = x.shape[2]
    return pl.pallas_call(
        functools.partial(body, boxes, True),
        out_shape=(jax.ShapeDtypeStruct((boxes, RANK, 512), BF16),
                   jax.ShapeDtypeStruct((boxes, RANK, RANK), BF16)),
        in_specs=[pl.BlockSpec(memory_space=pltpu.VMEM)] * 2,
        out_specs=[pl.BlockSpec(memory_space=pltpu.VMEM)] * 2,
        scratch_shapes=[pltpu.VMEM((boxes, RANK, 512), F32), pltpu.VMEM((boxes, RANK, RANK), F32)],
        compiler_params=pltpu.CompilerParams(vmem_limit_bytes=48 << 20),
    )(x, s)


def level2(x, s, dt):
    boxes = x.shape[1]
    return pl.pallas_call(
        functools.partial(body, boxes, False),
        out_shape=(jax.ShapeDtypeStruct((4, boxes, RANK, RANK), dt),
                   jax.ShapeDtypeStruct((boxes, RANK, RANK), dt)),
        in_specs=[pl.BlockSpec(memory_space=pltpu.VMEM)] * 2,
        out_specs=[pl.BlockSpec(memory_space=pltpu.VMEM)] * 2,
        scratch_shapes=[pltpu.VMEM((boxes, RANK, 512), F32), pltpu.VMEM((boxes, RANK, RANK), F32)],
        compiler_params=pltpu.CompilerParams(vmem_limit_bytes=48 << 20),
    )(x, s)


def shards(samples, sketch):
    parts = lax.axis_size("sample")
    columns = samples.shape[1]
    boxes = samples.shape[0] // (4 * parts * RANK)
    x = samples.reshape(2, 2, parts, boxes, RANK, columns)
    x = jnp.swapaxes(x, 1, 2).reshape(2 * parts, 2 * boxes, RANK, columns)
    x = lax.all_to_all(x, ("hi", "sample"), 0, 0, tiled=True)
    first, far = level1(x.reshape(2, parts, 2 * boxes, RANK, columns), sketch[0])
    far = lax.all_gather(far, "sample")
    far = jnp.swapaxes(far.reshape(parts, 2, boxes, RANK, RANK), 0, 1)
    far = far.reshape(2 * parts * boxes, RANK, RANK).astype(F32)
    x = lax.all_to_all(first.reshape(2, boxes, RANK, -1), "lo", 0, 0, tiled=True)
    basis, near = level2(x, sketch[1], BF16)
    near = lax.all_gather(near, "sample", tiled=True).astype(F32)
    basis = lax.all_to_all(basis, "sample", 0, 0, tiled=True)
    basis = basis.reshape(parts * boxes * RANK, columns).astype(F32)
    return (far, near, basis)


def solution(mesh):
    level, parts = mesh.devices.shape
    cut = Mesh(mesh.devices.reshape(2, level // 4, 2, parts), ("hi", "mid", "lo", "sample"))
    rows = ("hi", "mid", "lo")
    return jax.shard_map(
        shards,
        mesh=cut,
        in_specs=(P(rows, "sample"), P()),
        out_specs=(P(rows, None, None), P(rows, None, None), P(rows, "sample")),
        check_vma=False,
    )
```

```python
import functools
import math
import jax
import jax.numpy as jnp
from jax import lax
from jax.experimental import pallas as pl
from jax.experimental.pallas import tpu as pltpu
from jax.sharding import Mesh, PartitionSpec as P

RANK = 128
B = 32
EARLY = 2
FAR = 1
NEAR = 8_000_000_000
TURN = 1
F32 = jnp.float32
BF16 = jnp.bfloat16


def split3(x):
    h = x.astype(BF16)
    r = x - h.astype(F32)
    m = r.astype(BF16)
    l = (r - m.astype(F32)).astype(BF16)
    return h, m, l


def dot_nn(a, b):
    return lax.dot_general(a, b, (((1,), (0,)), ((), ())), preferred_element_type=F32)


def dot_nt(a, b):
    return lax.dot_general(a, b, (((1,), (1,)), ((), ())), preferred_element_type=F32)


def take_lanes(x, index):
    return jnp.take_along_axis(x, index, axis=1)


def leaf(rows, lane, sub):
    parts = B // 8
    scaled, full, low, out = [], [], [], None
    for i in range(B):
        mine, at = divmod(i, 8)
        here = sub == at
        row = []
        for g in range(parts):
            if g < mine:
                value = None
                for k in range(8 * g, i):
                    term = scaled[k][mine][at:at + 1, :] * (low[k] if k // 8 == g else full[k][g])
                    value = -term if value is None else value - term
            else:
                value = rows[i][g]
                for k in range(i):
                    if g == mine and k // 8 == g:
                        value = jnp.where(sub == k % 8, 0.0, value)
                    value = value - scaled[k][mine][at:at + 1, :] * full[k][g]
            row.append(value)
        r = lax.rsqrt(row[mine][at:at + 1, :])
        u = [part * r for part in row]
        scaled.append(u)
        done = list(u)
        done[mine] = jnp.where(here, r, u[mine])
        full.append(done)
        low.append(jnp.where(sub <= at, done[mine], 0.0))
        if i == 0:
            out = done
        else:
            chosen = (lane % B) == i
            out = [jnp.where(chosen, done[g], out[g]) for g in range(parts)]
    return out


def side(parts, q, order):
    h, m, l = (v.astype(F32) for v in parts)
    first = jnp.where((q == 0) | (q == order), h, m)
    second = jnp.where(q == 0, h if order == 1 else l, jnp.where(q == 1, l if order == 1 else h, 0.0))
    return jnp.concatenate([first.astype(BF16), second.astype(BF16)], axis=1)


def factor(f_refs, boxes):
    lane = lax.broadcasted_iota(jnp.int32, (8, RANK), 1)
    sub = lax.broadcasted_iota(jnp.int32, (8, RANK), 0)
    row_big = lax.broadcasted_iota(jnp.int32, (RANK, RANK), 0)
    lane_big = lax.broadcasted_iota(jnp.int32, (RANK, RANK), 1)
    row_block = lax.broadcasted_iota(jnp.int32, (B, RANK), 0)
    lane_block = lax.broadcasted_iota(jnp.int32, (B, RANK), 1)
    q_big, seg, parts = lane_big // B, lane // B, B // 8
    for p in range(RANK // B):
        lo = B * p
        cat = [None] * parts
        for b in range(boxes):
            for t in range(parts):
                tile = f_refs[b][lo + 8 * t:lo + 8 * t + 8, :]
                rep = take_lanes(tile, lo + lane % B)
                cat[t] = rep if b == 0 else jnp.where(seg % boxes == b, rep, cat[t])
        rows = []
        for i in range(B):
            rows.append([take_lanes(cat[t], seg * B + i) if t >= i // 8 else None for t in range(parts)])
        out = leaf(rows, lane, sub)
        for b in range(boxes):
            full = jnp.concatenate([take_lanes(out[t], b * B + lane % B) for t in range(parts)], axis=0)
            wt = jnp.where(row_block <= lane_block % B, full, 0.0)
            th, tm, tl = split3(wt)
            none = jnp.zeros((B, RANK), BF16)
            stack = jnp.concatenate([th, tm, th, tm, tl, th, none, none], axis=0)
            old = f_refs[b][...]
            wide = take_lanes(old, lo + lane_big % B)
            prod = dot_nn(side(split3(wide), q_big, 1), stack)
            above = [prod[:lo]] if lo else []
            below = [prod[lo + B:]] if lo + B < RANK else []
            base = jnp.where(q_big == p, jnp.concatenate(above + [full] + below, axis=0), old)
            if below:
                panel = jnp.concatenate(above + [wt] + below, axis=0)
                own = (row_big >= lo) & (row_big < lo + B) & (q_big > p)
                x = side(split3(panel), q_big, 1)
                y = side(split3(jnp.where(row_big >= lo + B, panel, 0.0)), q_big, 2)
                base = jnp.where(own, 0.0, base) - dot_nt(x, y)
            f_refs[b][...] = base


def project(boxes, pair, s_ref, z_ref, f_ref):
    s = s_ref[...]
    for b in range(boxes):
        for c in range(512 // RANK):
            z_ref[b, :, c * RANK:(c + 1) * RANK] = dot_nn(s, jnp.concatenate(pair(c, b), axis=0))
        h, m, l = split3(z_ref[b])
        hm = jnp.concatenate([h, m], axis=0)
        p1 = dot_nt(h, hm)
        p2 = dot_nt(m, hm)
        g = p1[:, :RANK] + ((p1[:, RANK:] + p2[:, :RANK]) + (dot_nt(l, h) + dot_nt(h, l)) + p2[:, RANK:])
        f_ref[b] = g
    factor([f_ref.at[b] for b in range(boxes)], boxes)


def results(b, z_ref, f_ref):
    row = lax.broadcasted_iota(jnp.int32, (RANK, RANK), 0)
    col = lax.broadcasted_iota(jnp.int32, (RANK, RANK), 1)
    f = f_ref[b]
    low = jnp.where(row > col, f, jnp.where(row == col, 1.0 / f, 0.0)).astype(BF16)
    w = jnp.where(row <= col, f, 0.0).T * math.sqrt(512)
    wh, wm, wl = split3(w)
    zh, zm, zl = split3(z_ref[b])
    q = dot_nn(jnp.concatenate([wh, wm], axis=1), jnp.concatenate([zh, zh], axis=0))
    q += dot_nn(wh, zm)
    return low, q.astype(BF16)


def far_body(boxes, early, here_ref, *refs):
    s_ref, given_ref, kept_ref, l_ref, z_ref, f_ref = refs[-6:]
    late = boxes - early

    def pair(c, b):
        received = refs[0][c, b] if b < early else refs[-7][c, b - early]
        return [here_ref[c, late + b], received]

    project(boxes, pair, s_ref, z_ref, f_ref)
    half = boxes // 2
    for b in range(boxes):
        low, q = results(b, z_ref, f_ref)
        for c in range(512 // RANK):
            l_ref[c, b] = low
        if b < half:
            given_ref[b] = q
        else:
            kept_ref[b - half] = q


def near_body(boxes, kept_ref, received_ref, s_ref, out_ref, z_ref, f_ref):
    def columns(c):
        return slice(c * RANK, (c + 1) * RANK)

    def pair(c, b):
        return [kept_ref[b, :, columns(c)], received_ref[b, :, columns(c)]]

    project(boxes, pair, s_ref, z_ref, f_ref)
    for b in range(boxes):
        low, q = results(b, z_ref, f_ref)
        for c in range(512 // RANK):
            out_ref[c, b] = q[:, columns(c)]
            out_ref[c, boxes + b] = low


VMEM = pl.BlockSpec(memory_space=pltpu.VMEM)


def call(body, boxes, shapes, operands, cost):
    return pl.pallas_call(
        body,
        out_shape=tuple(jax.ShapeDtypeStruct(shape, BF16) for shape in shapes),
        in_specs=[VMEM] * len(operands),
        out_specs=(VMEM,) * len(shapes),
        scratch_shapes=[pltpu.VMEM((boxes, RANK, 512), F32), pltpu.VMEM((boxes, RANK, RANK), F32)],
        cost_estimate=pl.CostEstimate(flops=cost, bytes_accessed=1 << 20, transcendentals=0),
        compiler_params=pltpu.CompilerParams(vmem_limit_bytes=40 << 20),
    )(*operands)


def turn_body(flag_ref, s_ref, first_ref, second_ref):
    for level, out_ref in enumerate((first_ref, second_ref)):
        s = s_ref[level]
        turned = jnp.concatenate([s[:, RANK:], s[:, :RANK]], axis=1)
        out_ref[...] = jnp.where(flag_ref[level] == 1, turned, s)


def turn(sketch, flags):
    shape = jax.ShapeDtypeStruct(sketch.shape[1:], sketch.dtype)
    return pl.pallas_call(
        turn_body,
        out_shape=(shape, shape),
        in_specs=[pl.BlockSpec(memory_space=pltpu.SMEM), VMEM],
        out_specs=(VMEM, VMEM),
        cost_estimate=pl.CostEstimate(flops=TURN, bytes_accessed=1 << 20, transcendentals=0),
    )(flags, sketch)


def flip(value, axis):
    return lax.ppermute(value, axis, [(0, 1), (1, 0)])


def shared(value):
    return lax.all_to_all(value, "sample", 0, 0, tiled=True)


def shards(samples, sketch):
    parts = lax.axis_size("sample")
    columns = samples.shape[1]
    quarter = samples.shape[0] // 4
    half = quarter // (parts * RANK)
    boxes = 2 * half
    up1, up2 = lax.axis_index("hi"), lax.axis_index("lo")

    def rows(side, part):
        taken = lax.dynamic_slice_in_dim(samples, (2 * side + part) * quarter, quarter, 0)
        return taken.reshape(parts, half, RANK, columns)

    given = jnp.concatenate([rows(1 - up1, 1 - up2), rows(1 - up1, up2)], axis=1)
    kept = jnp.concatenate([rows(up1, 1 - up2), rows(up1, up2)], axis=1)
    first = flip(given[:, :EARLY], "hi") if EARLY else None
    here = shared(jnp.concatenate([given[:, EARLY:], kept], axis=1))
    moved = [flip(here[:, :boxes - EARLY], "hi")] if EARLY < boxes else []
    if EARLY:
        moved.insert(0, shared(first))
    s1, s2 = turn(sketch, jnp.stack([up1, up2]).astype(jnp.int32))
    shape = (half, RANK, parts * columns)
    q_given, q_kept, far = call(
        functools.partial(far_body, boxes, EARLY), boxes, (shape, shape, (parts, boxes, RANK, RANK)), (here, *moved, s1), FAR)
    received = flip(q_given, "lo")
    far = shared(far)
    out = call(functools.partial(near_body, half), half, ((parts, boxes, RANK, RANK),), (q_kept, received, s2), NEAR)[0]
    out, far = lax.optimization_barrier((out, far))
    out = shared(out)
    basis = out[:, :half].reshape(parts * half * RANK, columns).astype(F32)
    near = out[:, half:].reshape(parts * half, RANK, RANK).astype(F32)
    l_given, l_kept = far[:, :half], far[:, half:]
    far = jnp.where(up2 == 1, jnp.stack([l_given, l_kept]), jnp.stack([l_kept, l_given])).astype(F32)
    return (far.reshape(2 * parts * half, RANK, RANK), near, basis)


def solution(mesh):
    level, parts = mesh.devices.shape
    cut = Mesh(mesh.devices.reshape(2, level // 4, 2, parts), ("hi", "mid", "lo", "sample"))
    rows = ("hi", "mid", "lo")
    return jax.shard_map(
        shards,
        mesh=cut,
        in_specs=(P(rows, "sample"), P()),
        out_specs=(P(rows, None, None), P(rows, None, None), P(rows, "sample")),
        check_vma=False,
    )
```

```python
import functools
import math
import jax
import jax.numpy as jnp
from jax import lax
from jax.experimental import pallas as pl
from jax.experimental.pallas import tpu as pltpu
from jax.sharding import Mesh, PartitionSpec as P

RANK = 128
B = 32
EARLY = 2
FAR = 1
NEAR = 8_000_000_000
F32 = jnp.float32
BF16 = jnp.bfloat16


def split3(x):
    h = x.astype(BF16)
    r = x - h.astype(F32)
    m = r.astype(BF16)
    l = (r - m.astype(F32)).astype(BF16)
    return h, m, l


def dot_nn(a, b):
    return lax.dot_general(a, b, (((1,), (0,)), ((), ())), preferred_element_type=F32)


def dot_nt(a, b):
    return lax.dot_general(a, b, (((1,), (1,)), ((), ())), preferred_element_type=F32)


def take_lanes(x, index):
    return jnp.take_along_axis(x, index, axis=1)


def leaf(rows, lane, sub):
    parts = B // 8
    scaled, full, low, out = [], [], [], None
    for i in range(B):
        mine, at = divmod(i, 8)
        here = sub == at
        row = []
        for g in range(parts):
            if g < mine:
                value = None
                for k in range(8 * g, i):
                    term = scaled[k][mine][at:at + 1, :] * (low[k] if k // 8 == g else full[k][g])
                    value = -term if value is None else value - term
            else:
                value = rows[i][g]
                for k in range(i):
                    if g == mine and k // 8 == g:
                        value = jnp.where(sub == k % 8, 0.0, value)
                    value = value - scaled[k][mine][at:at + 1, :] * full[k][g]
            row.append(value)
        r = lax.rsqrt(row[mine][at:at + 1, :])
        u = [part * r for part in row]
        scaled.append(u)
        done = list(u)
        done[mine] = jnp.where(here, r, u[mine])
        full.append(done)
        low.append(jnp.where(sub <= at, done[mine], 0.0))
        if i == 0:
            out = done
        else:
            chosen = (lane % B) == i
            out = [jnp.where(chosen, done[g], out[g]) for g in range(parts)]
    return out


def side(parts, q, order):
    h, m, l = (v.astype(F32) for v in parts)
    first = jnp.where((q == 0) | (q == order), h, m)
    second = jnp.where(q == 0, h if order == 1 else l, jnp.where(q == 1, l if order == 1 else h, 0.0))
    return jnp.concatenate([first.astype(BF16), second.astype(BF16)], axis=1)


def factor(f_refs, boxes):
    lane = lax.broadcasted_iota(jnp.int32, (8, RANK), 1)
    sub = lax.broadcasted_iota(jnp.int32, (8, RANK), 0)
    row_big = lax.broadcasted_iota(jnp.int32, (RANK, RANK), 0)
    lane_big = lax.broadcasted_iota(jnp.int32, (RANK, RANK), 1)
    row_block = lax.broadcasted_iota(jnp.int32, (B, RANK), 0)
    lane_block = lax.broadcasted_iota(jnp.int32, (B, RANK), 1)
    q_big, seg, parts = lane_big // B, lane // B, B // 8
    for p in range(RANK // B):
        lo = B * p
        cat = [None] * parts
        for b in range(boxes):
            for t in range(parts):
                tile = f_refs[b][lo + 8 * t:lo + 8 * t + 8, :]
                rep = take_lanes(tile, lo + lane % B)
                cat[t] = rep if b == 0 else jnp.where(seg % boxes == b, rep, cat[t])
        rows = []
        for i in range(B):
            rows.append([take_lanes(cat[t], seg * B + i) if t >= i // 8 else None for t in range(parts)])
        out = leaf(rows, lane, sub)
        for b in range(boxes):
            full = jnp.concatenate([take_lanes(out[t], b * B + lane % B) for t in range(parts)], axis=0)
            wt = jnp.where(row_block <= lane_block % B, full, 0.0)
            th, tm, tl = split3(wt)
            none = jnp.zeros((B, RANK), BF16)
            stack = jnp.concatenate([th, tm, th, tm, tl, th, none, none], axis=0)
            old = f_refs[b][...]
            wide = take_lanes(old, lo + lane_big % B)
            prod = dot_nn(side(split3(wide), q_big, 1), stack)
            above = [prod[:lo]] if lo else []
            below = [prod[lo + B:]] if lo + B < RANK else []
            base = jnp.where(q_big == p, jnp.concatenate(above + [full] + below, axis=0), old)
            if below:
                panel = jnp.concatenate(above + [wt] + below, axis=0)
                own = (row_big >= lo) & (row_big < lo + B) & (q_big > p)
                x = side(split3(panel), q_big, 1)
                y = side(split3(jnp.where(row_big >= lo + B, panel, 0.0)), q_big, 2)
                base = jnp.where(own, 0.0, base) - dot_nt(x, y)
            f_refs[b][...] = base


def project(boxes, pair, flag_ref, s_ref, z_ref, f_ref):
    s = s_ref[...]
    s = jnp.where(flag_ref[0] == 1, jnp.concatenate([s[:, RANK:], s[:, :RANK]], axis=1), s)
    for b in range(boxes):
        for c in range(512 // RANK):
            z_ref[b, :, c * RANK:(c + 1) * RANK] = dot_nn(s, jnp.concatenate(pair(c, b), axis=0))
        h, m, l = split3(z_ref[b])
        hm = jnp.concatenate([h, m], axis=0)
        p1 = dot_nt(h, hm)
        p2 = dot_nt(m, hm)
        g = p1[:, :RANK] + ((p1[:, RANK:] + p2[:, :RANK]) + (dot_nt(l, h) + dot_nt(h, l)) + p2[:, RANK:])
        f_ref[b] = g
    factor([f_ref.at[b] for b in range(boxes)], boxes)


def results(b, z_ref, f_ref):
    row = lax.broadcasted_iota(jnp.int32, (RANK, RANK), 0)
    col = lax.broadcasted_iota(jnp.int32, (RANK, RANK), 1)
    f = f_ref[b]
    low = jnp.where(row > col, f, jnp.where(row == col, 1.0 / f, 0.0)).astype(BF16)
    w = jnp.where(row <= col, f, 0.0).T * math.sqrt(512)
    wh, wm, wl = split3(w)
    zh, zm, zl = split3(z_ref[b])
    q = dot_nn(jnp.concatenate([wh, wm], axis=1), jnp.concatenate([zh, zh], axis=0))
    q += dot_nn(wh, zm)
    return low, q.astype(BF16)


def far_body(boxes, early, here_ref, *refs):
    flag_ref, s_ref, given_ref, kept_ref, l_ref, z_ref, f_ref = refs[-7:]
    late = boxes - early

    def pair(c, b):
        received = refs[0][c, b] if b < early else refs[-8][c, b - early]
        return [here_ref[c, late + b], received]

    project(boxes, pair, flag_ref, s_ref, z_ref, f_ref)
    half = boxes // 2
    for b in range(boxes):
        low, q = results(b, z_ref, f_ref)
        for c in range(512 // RANK):
            l_ref[c, b] = low
        if b < half:
            given_ref[b] = q
        else:
            kept_ref[b - half] = q


def near_body(boxes, kept_ref, received_ref, flag_ref, s_ref, out_ref, z_ref, f_ref):
    def columns(c):
        return slice(c * RANK, (c + 1) * RANK)

    def pair(c, b):
        return [kept_ref[b, :, columns(c)], received_ref[b, :, columns(c)]]

    project(boxes, pair, flag_ref, s_ref, z_ref, f_ref)
    for b in range(boxes):
        low, q = results(b, z_ref, f_ref)
        for c in range(512 // RANK):
            out_ref[c, b] = q[:, columns(c)]
            out_ref[c, boxes + b] = low


VMEM = pl.BlockSpec(memory_space=pltpu.VMEM)


def call(body, boxes, shapes, operands, cost):
    return pl.pallas_call(
        body,
        out_shape=tuple(jax.ShapeDtypeStruct(shape, BF16) for shape in shapes),
        in_specs=[VMEM] * (len(operands) - 2) + [pl.BlockSpec(memory_space=pltpu.SMEM), VMEM],
        out_specs=(VMEM,) * len(shapes),
        scratch_shapes=[pltpu.VMEM((boxes, RANK, 512), F32), pltpu.VMEM((boxes, RANK, RANK), F32)],
        cost_estimate=pl.CostEstimate(flops=cost, bytes_accessed=1 << 20, transcendentals=0),
        compiler_params=pltpu.CompilerParams(vmem_limit_bytes=40 << 20),
    )(*operands)


def flip(value, axis):
    return lax.ppermute(value, axis, [(0, 1), (1, 0)])


def shared(value):
    return lax.all_to_all(value, "sample", 0, 0, tiled=True)


def shards(samples, sketch):
    parts = lax.axis_size("sample")
    columns = samples.shape[1]
    quarter = samples.shape[0] // 4
    half = quarter // (parts * RANK)
    boxes = 2 * half
    up1, up2 = lax.axis_index("hi"), lax.axis_index("lo")

    def rows(side, part):
        taken = lax.dynamic_slice_in_dim(samples, (2 * side + part) * quarter, quarter, 0)
        return taken.reshape(parts, half, RANK, columns)

    given = jnp.concatenate([rows(1 - up1, 1 - up2), rows(1 - up1, up2)], axis=1)
    kept = jnp.concatenate([rows(up1, 1 - up2), rows(up1, up2)], axis=1)
    first = flip(given[:, :EARLY], "hi") if EARLY else None
    here = shared(jnp.concatenate([given[:, EARLY:], kept], axis=1))
    moved = [flip(here[:, :boxes - EARLY], "hi")] if EARLY < boxes else []
    if EARLY:
        moved.insert(0, shared(first))
    f1, f2 = up1.astype(jnp.int32)[None], up2.astype(jnp.int32)[None]
    shape = (half, RANK, parts * columns)
    q_given, q_kept, far = call(
        functools.partial(far_body, boxes, EARLY), boxes, (shape, shape, (parts, boxes, RANK, RANK)), (here, *moved, f1, sketch[0]), FAR)
    received = flip(q_given, "lo")
    far = shared(far)
    out = call(functools.partial(near_body, half), half, ((parts, boxes, RANK, RANK),), (q_kept, received, f2, sketch[1]), NEAR)[0]
    out, far = lax.optimization_barrier((out, far))
    out = shared(out)
    basis = out[:, :half].reshape(parts * half * RANK, columns).astype(F32)
    near = out[:, half:].reshape(parts * half, RANK, RANK).astype(F32)
    l_given, l_kept = far[:, :half], far[:, half:]
    far = jnp.where(up2 == 1, jnp.stack([l_given, l_kept]), jnp.stack([l_kept, l_given])).astype(F32)
    return (far.reshape(2 * parts * half, RANK, RANK), near, basis)


def solution(mesh):
    level, parts = mesh.devices.shape
    cut = Mesh(mesh.devices.reshape(2, level // 4, 2, parts), ("hi", "mid", "lo", "sample"))
    rows = ("hi", "mid", "lo")
    return jax.shard_map(
        shards,
        mesh=cut,
        in_specs=(P(rows, "sample"), P()),
        out_specs=(P(rows, None, None), P(rows, None, None), P(rows, "sample")),
        check_vma=False,
    )
```
